32 devices in a mesh: pole: 4 (over y, x), blk: 8 (over z, core).
Axes of the slice: x: 2, y: 2, z: 4, core: 2. Of those that a mesh axis runs over, the one named last changes fastest.
Arguments:
- inverse_block: float32 [4, 2, 4096, 4096], P('pole', None, 'blk'), may hold values from -0.09375 to 0.09375
- factor: float32 [4, 4096, 2, 512], P('pole', 'blk'), may hold values from -0.75 to 0.75
- diag_inverse: float32 [4, 2, 2, 256, 256], P('pole', None, None, 'blk'), may hold values from -6 to 6
- pole_weight: float32 [4, 2], P('pole'), may hold values from -4 to 4
- block_ids: int32 [32, 8], P(('pole', 'blk')), may hold values from 0 to 31, as said below
- block_count: int32 [32], P(('pole', 'blk')), may hold values from 1 to 8, 144 in all
- basis: float32 [32, 2048, 1024], P(('pole', 'blk')), may hold values from -0.1875 to 0.1875
- column_basis: float32 [32, 2048, 512], P(('pole', 'blk')), may hold values from -0.25 to 0.25
Outputs:
- diag_density: float32 [2, 256, 256], P(None, 'blk')
- density: float32 [32, 2048], P(('pole', 'blk'))
The draws below stay inside these ranges and needn't reach their ends.
Inputs may be any that keep to these rules, and one draw needn't show every extreme that they name: Entries of block_ids beyond a batch's block_count are not read; block_count reaches 8 in every draw. With b = g mod 8, every entry of block_ids[g] names a block of rows b' * 4096 // 8 to (b' + 1) * 4096 // 8 for some b' between b - 2 and b + 2.
All inputs are finite; a program needn't handle non-finite values. No bound on the sum of `block_count` on one device may be relied on, other than what follows from the above.
Results may differ from the reference program's by a relative error of at most 0.0003.
Values sent between devices are 32-bit elements; how exact they have to be, the bound alone decides.
No kernel may reach another device: no remote copies, remote signals or barrier semaphores. Data moves between devices by JAX's collectives and lax.ppermute only.
A program may use at most 128 MiB of HBM per device.

```python
import math
import jax
import jax.numpy as jnp
import numpy as np
from jax import lax

M = 4096
K = 256
UPD = 2
RB = 128
MOST = 8
REACH = 2
PTS = 2048
POLES = 4
NBATCH = 32
COLS = 512
N_BLK = 8


def draw_block_ids(key, part):
    batch = jnp.arange(NBATCH, dtype=jnp.int32)[:, None]
    place = batch % N_BLK
    per_device = M // N_BLK // RB
    lowest = jnp.maximum(place - REACH, 0) * per_device
    highest = jnp.minimum(place + REACH + 1, N_BLK) * per_device
    raw = jax.random.randint(key, (NBATCH, MOST), 0, 1048576, dtype=jnp.int32)
    return (lowest + raw % (highest - lowest)).astype(jnp.int32)


def block_scale(stream_key, shape, split, low, high):
    level, own = 1.0, jax.random.fold_in(stream_key, 6)
    for dim, blocks in split:
        draws = jnp.exp(jax.random.uniform(jax.random.fold_in(own, dim), (blocks,), jnp.float32, low / len(split), high / len(split)))
        level = level * jnp.repeat(draws, shape[dim] // blocks).reshape([-1 if axis == dim else 1 for axis in range(len(shape))])
    return level


def split_up(count, total, reach, skew):
    loads = [(1 << 20) // math.isqrt(grade ** skew) + 1 for grade in range(2, count + 1)]
    surplus, given = total - reach - (count - 1), [1] * (count - 1)
    while surplus > 0:
        candidates = [i for i in range(count - 1) if given[i] < reach]
        mass, left = sum([loads[i] for i in candidates]), surplus
        for i in candidates:
            addition = min(reach - given[i], max(1, left * loads[i] // mass), surplus)
            given[i] = given[i] + addition
            surplus = surplus - addition
    return np.array([reach] + given)


def uneven(stream_key, count, total, bound, lean):
    if count == 2:
        one = jax.random.randint(stream_key, (), max(1, total - bound), min(bound, total - 1) + 1)
        return jnp.stack([one, total - one])
    tallies = jnp.asarray(split_up(count, total, bound, lean), jnp.int32)
    twos = (count - 1) // 2
    giver, sink = tallies[1:1 + 2 * twos:2], tallies[2:2 + 2 * twos:2]
    slack = jnp.minimum(giver - 1, bound - sink)
    passed = jax.random.randint(jax.random.fold_in(stream_key, 1), (twos,), 0, 1 << 20) % (slack + 1)
    tallies = tallies.at[1:1 + 2 * twos:2].set(giver - passed).at[2:2 + 2 * twos:2].set(sink + passed)
    return tallies[jax.random.permutation(jax.random.fold_in(stream_key, 2), count)]


def noise(key, shape, scale, reach, cuts=(), held_as=jnp.bfloat16):
    gain = block_scale(key, shape, cuts, -0.22, 0.18) if cuts else 1.0
    result = jax.random.normal(key, shape, jnp.float32) * scale * gain
    return jnp.minimum(jnp.maximum(result, -reach), reach).astype(held_as)


def setup_inputs(seed: int = 0) -> dict:
    key_list = jax.random.split(jax.random.key(seed), 9)
    inverse_block = noise(key_list[0], (POLES, 2, M, M), M ** -0.5, 0.09375, ((0, 4), (2, 8)), jnp.float32)
    factor = noise(key_list[1], (POLES, M, 2, COLS), 0.125, 0.75, ((0, 4), (1, 8)), jnp.float32)
    diag_inverse = noise(key_list[2], (POLES, 2, UPD, K, K), 1.0, 6.0, ((0, 4), (3, 8)), jnp.float32)
    pole_weight = noise(key_list[3], (POLES, 2), 1.0, 4.0, ((0, 4),), jnp.float32)
    block_ids = draw_block_ids(jax.random.fold_in(key_list[8], 71), 0)
    block_count = uneven(key_list[5], NBATCH, NBATCH * (MOST + 1) // 2, MOST, 2).astype(jnp.int32)
    basis = noise(key_list[6], (NBATCH, PTS, MOST * RB), (MOST * RB) ** -0.5, 0.1875, ((0, 32),), jnp.float32)
    column_basis = noise(key_list[7], (NBATCH, PTS, COLS), COLS ** -0.5, 0.25, ((0, 32),), jnp.float32)
    return {"inverse_block": inverse_block, "factor": factor, "diag_inverse": diag_inverse, "pole_weight": pole_weight, "block_ids": block_ids, "block_count": block_count, "basis": basis, "column_basis": column_basis}


HIGH = lax.Precision.HIGHEST


def matmul(left, right):
    return jnp.dot(left, right, preferred_element_type=jnp.float32, precision=HIGH)


def pair(left, right):
    return jnp.einsum('mjk,mjl->jkl', left, right, precision=HIGH)


def per_pole(items):
    block, panel, diag, weight = items
    real_g, imag_g = block[0], block[1]
    real_l, imag_l = panel[:, 0, :], panel[:, 1, :]
    real_x = -(matmul(real_g, real_l) - matmul(imag_g, imag_l))
    imag_x = -(matmul(real_g, imag_l) + matmul(imag_g, real_l))
    real_l3 = real_l.reshape(M, UPD, K)
    imag_l3 = imag_l.reshape(M, UPD, K)
    real_x3 = real_x.reshape(M, UPD, K)
    imag_x3 = imag_x.reshape(M, UPD, K)
    real_c = pair(real_l3, real_x3) - pair(imag_l3, imag_x3)
    imag_c = pair(real_l3, imag_x3) + pair(imag_l3, real_x3)
    real_s = diag[0] - real_c
    imag_s = diag[1] - imag_c
    part_matrix = weight[0] * real_x - weight[1] * imag_x
    part_diag = weight[0] * real_s - weight[1] * imag_s
    return part_matrix, part_diag


def reference(inverse_block, factor, diag_inverse, pole_weight, block_ids, block_count, basis, column_basis):
    parts_matrix, parts_diag = lax.map(per_pole, (inverse_block, factor, diag_inverse, pole_weight))
    matrix = jnp.sum(parts_matrix, axis=0)
    diag_density = jnp.sum(parts_diag, axis=0)
    blocks = matrix.reshape(M // RB, RB, UPD * K)

    def per_batch(items):
        ids, count, values, columns = items
        chosen = blocks[ids.astype(jnp.int32)]
        keep = (jnp.arange(MOST, dtype=jnp.int32) < count).astype(jnp.float32)
        selected = (chosen * keep[:, None, None]).reshape(MOST * RB, UPD * K)
        product = matmul(values, selected)
        return jnp.sum(product * columns, axis=-1)

    density = lax.map(per_batch, (block_ids, block_count, basis, column_basis))
    return diag_density, density
```

```python
import functools

import jax
import jax.numpy as jnp
from jax import lax
from jax.experimental import pallas as pl
from jax.experimental.pallas import tpu as pltpu
from jax.sharding import PartitionSpec as P

REACH = 2
CORES = 2

HIGH = lax.Precision.HIGH
F32 = jnp.float32
BF16 = jnp.bfloat16


def halves(value):
    high = value.astype(BF16)
    low = (value - high.astype(F32)).astype(BF16)
    return high, low


def dot3(left, right):
    left_high, left_low = halves(left)
    right_high, right_low = halves(right)
    dot = functools.partial(jnp.dot, preferred_element_type=F32)
    return dot(left_high, right_high) + dot(left_high, right_low) + dot(left_low, right_high)


def panel_kernel(refs, steps, fresh, split, table, *args):
    g_ref = args[0]
    panels = args[1 : 1 + refs]
    args = args[1 + refs :]
    if not fresh:
        before, args = args[0], args[1:]
    if split:
        out_real, out_imag, total, held, sems = args
    else:
        total, held, sems = args
    slot = pl.program_id(0)
    part = pl.program_id(1)
    now = slot * steps + part
    last = pl.num_programs(0) * steps - 1
    rows = held.shape[1]
    cols = held.shape[2] // 2

    def fetch(at, act):
        place = at // steps
        start = pl.multiple_of((at % steps) * rows, rows)
        for i in range(refs):
            @pl.when(jnp.logical_and(table[0, place] == i, table[2, place] == 1))
            def _():
                copy = pltpu.make_async_copy(
                    panels[i].at[pl.ds(start, rows), :], held.at[at % 2], sems.at[at % 2]
                )
                act(copy)

    @pl.when(now == 0)
    def _():
        fetch(now, lambda copy: copy.start())
        if fresh:
            total[...] = jnp.zeros_like(total)
        else:
            total[...] = before[...]

    @pl.when(now < last)
    def _():
        fetch(now + 1, lambda copy: copy.start())

    fetch(now, lambda copy: copy.wait())

    @pl.when(table[2, slot] == 1)
    def _():
        panel = held[now % 2]
        real, imag = panel[:, :cols], panel[:, cols:]
        right = jnp.concatenate([panel, jnp.concatenate([-imag, real], axis=1)], axis=0)
        left = jnp.concatenate([g_ref[0, 0], g_ref[0, 1]], axis=1)
        total[...] += dot3(left, right)

    if split:
        @pl.when(now == last)
        def _():
            out_real[...] = total[:, :cols]
            out_imag[...] = total[:, cols:]


def add_panels(table, blocks, panels, before, split):
    rows = blocks.shape[2]
    depth, wide = panels[0].shape
    steps = 2
    slots = table.shape[1]
    g_spec = pl.BlockSpec(
        (1, 2, rows, depth // steps), lambda s, t, tab: (0, 0, 0, tab[1, s] * steps + t)
    )
    whole = pl.BlockSpec((rows, wide), lambda s, t, tab: (0, 0))
    half = pl.BlockSpec((rows, wide // 2), lambda s, t, tab: (0, 0))
    in_specs = [g_spec] + [pl.BlockSpec(memory_space=pl.ANY)] * len(panels)
    operands = [blocks, *panels]
    if before is not None:
        in_specs.append(whole)
        operands.append(before)
    if split:
        out_shape = [jax.ShapeDtypeStruct((rows, wide // 2), F32)] * 2
        out_specs = [half, half]
        scratch = [pltpu.VMEM((rows, wide), F32)]
    else:
        out_shape = jax.ShapeDtypeStruct((rows, wide), F32)
        out_specs = whole
        scratch = []
    scratch += [
        pltpu.VMEM((2, depth // steps, wide), F32),
        pltpu.SemaphoreType.DMA((2,)),
    ]
    kernel = functools.partial(panel_kernel, len(panels), steps, before is None, split)
    return pl.pallas_call(
        kernel,
        out_shape=out_shape,
        grid_spec=pltpu.PrefetchScalarGridSpec(
            num_scalar_prefetch=1,
            grid=(slots, steps),
            in_specs=in_specs,
            out_specs=out_specs,
            scratch_shapes=scratch,
        ),
        compiler_params=pltpu.CompilerParams(vmem_limit_bytes=24 << 20),
        cost_estimate=pl.CostEstimate(
            flops=slots * 3 * 2 * rows * 2 * depth * wide,
            bytes_accessed=slots * 4 * (2 * rows * depth + depth * wide),
            transcendentals=0,
        ),
        name="panels",
    )(table, *operands)


def density_kernel(refs, slots, table, basis_ref, column_ref, *args):
    windows = args[:refs]
    args = args[refs:]
    before, out_ref, chosen, high, low, sem = args
    size = chosen.shape[0] // slots

    def each(act):
        for s in range(slots):
            for i in range(refs):
                @pl.when(jnp.logical_and(table[0, s] == i, table[2, s] == 1))
                def _():
                    start = pl.multiple_of(table[1, s] * size, size)
                    act(
                        pltpu.make_async_copy(
                            windows[i].at[pl.ds(start, size), :],
                            chosen.at[pl.ds(s * size, size), :],
                            sem.at[s],
                        )
                    )

    @pl.when(pl.program_id(0) == 0)
    def _():
        each(lambda copy: copy.start())
        for s in range(slots):
            @pl.when(table[2, s] == 0)
            def _():
                chosen[pl.ds(s * size, size), :] = jnp.zeros((size, chosen.shape[1]), F32)
        each(lambda copy: copy.wait())
        high[...], low[...] = halves(chosen[...])

    dot = functools.partial(jnp.dot, preferred_element_type=F32)
    basis_high, basis_low = halves(basis_ref[0])
    product = dot(basis_high, high[...]) + dot(basis_high, low[...]) + dot(basis_low, high[...])
    terms = product * column_ref[0]
    lanes = 128
    folded = terms[:, :lanes]
    for start in range(lanes, terms.shape[1], lanes):
        folded = folded + terms[:, start : start + lanes]
    out_ref[...] = before[...] + jnp.sum(folded.T, axis=0, keepdims=True)


def add_density(table, basis, column_basis, windows, before, start):
    points, depth = basis.shape[1:]
    wide = windows[0].shape[1]
    slots = table.shape[1]
    tile = points // 8
    first = start // wide
    return pl.pallas_call(
        functools.partial(density_kernel, len(windows), slots),
        out_shape=jax.ShapeDtypeStruct((1, points), F32),
        grid_spec=pltpu.PrefetchScalarGridSpec(
            num_scalar_prefetch=1,
            grid=(points // tile,),
            in_specs=[
                pl.BlockSpec((1, tile, depth), lambda t, tab: (0, t, 0)),
                pl.BlockSpec((1, tile, wide), lambda t, tab: (0, t, first)),
            ]
            + [pl.BlockSpec(memory_space=pl.ANY)] * len(windows)
            + [pl.BlockSpec((1, tile), lambda t, tab: (0, t))],
            out_specs=pl.BlockSpec((1, tile), lambda t, tab: (0, t)),
            scratch_shapes=[
                pltpu.VMEM((depth, wide), F32),
                pltpu.VMEM((depth, wide), BF16),
                pltpu.VMEM((depth, wide), BF16),
                pltpu.SemaphoreType.DMA((slots,)),
            ],
        ),
        compiler_params=pltpu.CompilerParams(vmem_limit_bytes=24 << 20),
        cost_estimate=pl.CostEstimate(
            flops=3 * 2 * points * depth * wide,
            bytes_accessed=4 * points * (depth + wide),
            transcendentals=0,
        ),
        name="density",
    )(table, basis, column_basis, *windows, before)


def hop(value, distance, chips):
    route = [
        (CORES * (z - distance) + c, CORES * z + c)
        for z in chips
        for c in range(CORES)
    ]
    return lax.ppermute(value, "blk", route)


def across(value, chips):
    route = [(CORES * z + 1 - c, CORES * z + c) for z in chips for c in range(CORES)]
    return lax.ppermute(value, "blk", route)


def swap(value, axis, bit):
    route = [(i ^ bit, i) for i in range(lax.axis_size(axis))]
    return lax.ppermute(value, axis, route)


def bits(count):
    return [1 << i for i in range(count.bit_length() - 1)]


def body(
    inverse_block, factor, diag_inverse, pole_weight, block_ids, block_count, basis, column_basis
):
    rows = inverse_block.shape[2]
    cols = factor.shape[3]
    updates, width = diag_inverse.shape[2], diag_inverse.shape[4]
    poles = lax.axis_size("pole")
    chips = lax.axis_size("blk") // CORES
    place = lax.axis_index("blk")
    z, core = place // CORES, place % CORES
    weight_re, weight_im = pole_weight[0, 0], pole_weight[0, 1]
    real_l, imag_l = factor[0, :, 0, :], factor[0, :, 1, :]

    starts = [0, cols // 2, 3 * cols // 4]
    widths = [cols // 2, cols // 4, cols // 4]
    own = []
    for start, wide in zip(starts, widths):
        re, im = real_l[:, start : start + wide], imag_l[:, start : start + wide]
        own.append(
            jnp.concatenate(
                [weight_im * im - weight_re * re, -(weight_re * im) - weight_im * re], axis=1
            )
        )

    def table_of(entries):
        return jnp.stack([jnp.stack([jnp.asarray(v, jnp.int32) for v in row]) for row in zip(*entries)])

    every = range(chips)

    def gather(panel):
        partner = across(panel, every)
        mine, other = place, place + 1 - 2 * core
        stages = [([panel, partner], table_of([(0, mine, 1), (1, other, 1)]))]
        up = down = panel
        for s in range(1, chips):
            up = hop(up, 1, range(s, chips))
            down = hop(down, -1, range(0, chips - s))
            up_other = across(up, range(s, chips))
            down_other = across(down, range(0, chips - s))
            has_up = (z >= s).astype(jnp.int32)
            has_down = (z < chips - s).astype(jnp.int32)
            arrays = [up, up_other, down, down_other]
            low, high = CORES * (z - s), CORES * (z + s)
            if 2 * s <= chips - 1:
                entries = [
                    (0, jnp.maximum(low + core, 0), has_up),
                    (1, jnp.maximum(low + 1 - core, 0), has_up),
                    (2, jnp.minimum(high + core, CORES * chips - 1), has_down),
                    (3, jnp.minimum(high + 1 - core, CORES * chips - 1), has_down),
                ]
            else:
                source = jnp.where(has_up == 1, low, jnp.where(has_down == 1, high, 0))
                which = 2 * (1 - has_up)
                valid = has_up + has_down
                entries = [
                    (which, source + core, valid),
                    (which + 1, source + 1 - core, valid),
                ]
            stages.append((arrays, table_of(entries)))
        return stages

    per_device = rows * CORES * chips // (CORES * chips)
    slots = block_ids.shape[1]
    size = basis.shape[2] // slots
    each = per_device // size
    ids = block_ids[0]
    device = ids // each
    offset = device // CORES - z + 1
    other = (device % CORES != core).astype(jnp.int32)
    used = (jnp.arange(slots, dtype=jnp.int32) < block_count[0]).astype(jnp.int32)
    pick = jnp.stack([3 * other + offset, ids % each, used])

    density = jnp.zeros((1, basis.shape[1]), F32)
    crossed = []
    stages = [gather(panel) for panel in own]
    for start, wide, chunk in zip(starts, widths, stages):
        total = None
        for i, (arrays, table) in enumerate(chunk):
            total = add_panels(table, inverse_block, arrays, total, i == len(chunk) - 1)
        real_y, imag_y = total
        update = start // width
        contract = (((0,), (0,)), ((), ()))
        re = real_l[:, update * width : (update + 1) * width]
        im = imag_l[:, update * width : (update + 1) * width]
        crossed.append(
            lax.dot_general(re, real_y, contract, precision=HIGH)
            - lax.dot_general(im, imag_y, contract, precision=HIGH)
        )
        for bit in bits(poles):
            real_y = real_y + swap(real_y, "pole", bit)
        below = hop(real_y, 1, range(1, chips))
        above = hop(real_y, -1, range(0, chips - 1))
        windows = [below, real_y, above]
        windows += [across(below, range(1, chips)), across(real_y, every), across(above, range(0, chips - 1))]
        density = add_density(pick, basis, column_basis, windows, density, start)

    whole = jnp.concatenate(crossed, axis=1).reshape(width, updates, width)
    keep = jnp.moveaxis(whole, 1, 0).reshape(updates, chips, CORES, width // (CORES * chips), width)

    def shrink(value, axis, bit, index):
        mine = lax.dynamic_index_in_dim(value, index, axis, keepdims=False)
        sent = lax.dynamic_index_in_dim(value, 1 - index, axis, keepdims=False)
        return mine + swap(sent, "blk", bit)

    keep = shrink(keep, 2, 1, core)
    for bit in bits(chips):
        high = keep.shape[1] // 2
        keep = keep.reshape((updates, high, 2) + keep.shape[2:])
        keep = shrink(keep, 2, CORES * bit, (z // bit) % 2)
    keep = keep.reshape(updates, width // (CORES * chips), width)
    diag = weight_re * diag_inverse[0, 0] - weight_im * diag_inverse[0, 1] - keep
    for bit in bits(poles):
        diag = diag + swap(diag, "pole", bit)
    return (diag, density)


def solution(mesh):
    in_specs = (
        P("pole", None, "blk", None),
        P("pole", "blk", None, None),
        P("pole", None, None, "blk", None),
        P("pole", None),
        P(("pole", "blk"), None),
        P(("pole", "blk")),
        P(("pole", "blk"), None, None),
        P(("pole", "blk"), None, None),
    )
    out_specs = (P(None, "blk", None), P(("pole", "blk"), None))
    return jax.shard_map(body, mesh=mesh, in_specs=in_specs, out_specs=out_specs, check_vma=False)
```
